512 devices in a mesh: resp: 32 (over x, y), mp: 16 (over z, core).
Axes of the slice: x: 4, y: 8, z: 8, core: 2. Of those that a mesh axis runs over, the one named last changes fastest.
Arguments:
- queries: bfloat16 [32, 512, 4096], P('resp', None, 'mp'), may hold values from -160 to 160
- keys: bfloat16 [32, 512, 512], P('resp'), may hold values from -8 to 8
- values: bfloat16 [32, 512, 512], P('resp'), may hold values from -6 to 6
- out_weight: bfloat16 [4096, 8192], P(None, 'mp'), may hold values from -1.5 to 1.5
- order_bias: float32 [2, 32], replicated, may hold values from -2 to 2
- partners: int32 [32, 6], P('resp'), may hold values from -1 to 31, as said below
- count: int32 [32], P('resp'), may hold values from 1 to 6, as said below
- order: int32 [32, 6], P('resp'), may hold values 0 or 1
Outputs:
- judged: bfloat16 [32, 512, 8192], P('resp', None, 'mp')
The draws below stay inside these ranges and needn't reach their ends.
Inputs may be any that keep to these rules, and one draw needn't show every extreme that they name: `partners`: slot s of response r is used iff s < count[r]; unused slots hold -1; a used entry names a response other than r at cyclic distance at most 3; the used entries of a row are distinct. `count`: some response has 6 partners and some other has 1.
All inputs are finite; a program needn't handle non-finite values. No bound on the sum of `order` on one device may be relied on, other than what follows from the above.
Results may differ from the reference program's by a relative error of at most 0.0057.
Values may be sent and summed in bfloat16 or wider, within the bound.
A program may use at most 64 MiB of HBM per device.

```python
import math
import jax
import jax.numpy as jnp
from jax import lax

D = 8192
HQ = 32
KVH = 4
HD = 128
LEN = 512
REACH = 3
SLOTS = 6
RESPONSES = 32


def links(key):
    base_key = jax.random.fold_in(key, 7)
    key_count, key_full, key_sparse, key_perm = jax.random.split(base_key, 4)
    counts = jax.random.randint(key_count, (RESPONSES,), 1, SLOTS + 1)
    fullest = jax.random.randint(key_full, (), 0, RESPONSES)
    sparsest = (fullest + 1 + jax.random.randint(key_sparse, (), 0, RESPONSES - 1)) % RESPONSES
    counts = counts.at[fullest].set(SLOTS).at[sparsest].set(1)
    offsets = jnp.concatenate([jnp.arange(1, REACH + 1), -jnp.arange(1, REACH + 1)]).astype(jnp.int32)
    row_keys = jax.random.split(key_perm, RESPONSES)
    shuffled = jax.vmap(lambda row_key: jax.random.permutation(row_key, offsets))(row_keys)
    row_ids = jnp.arange(RESPONSES, dtype=jnp.int32)[:, None]
    targets = (row_ids + shuffled) % RESPONSES
    in_use = jnp.arange(SLOTS, dtype=jnp.int32)[None, :] < counts[:, None]
    partner_ids = jnp.where(in_use, targets, -1)
    return (partner_ids.astype(jnp.int32), counts.astype(jnp.int32))


def draw_partners(key, part):
    return links(key)[0]


def draw_count(key, part):
    return links(key)[1]


def features(key):
    base_key = jax.random.fold_in(key, 3)
    key_query, key_key = jax.random.split(base_key)
    query_rows = jnp.clip(jax.random.normal(key_query, (RESPONSES, LEN, HQ * HD), jnp.float32), -6.0, 6.0)
    key_rows = jnp.clip(jax.random.normal(key_key, (RESPONSES, LEN, KVH * HD), jnp.float32), -6.0, 6.0)
    return (query_rows, key_rows)


def draw_queries(key, part):
    return features(key)[0].astype(jnp.bfloat16)


def draw_keys(key, part):
    return features(key)[1].astype(jnp.bfloat16)


def set_ends(result, own_key, low, top_value):
    place = [jax.random.randint(jax.random.fold_in(own_key, axis), (), 0, length) for axis, length in enumerate(result.shape)]
    longest = result.shape.index(max(result.shape))
    beside = place[:longest] + [(place[longest] + 1) % result.shape[longest]] + place[longest + 1:]
    return result.at[tuple(place)].set(low).at[tuple(beside)].set(top_value)


def level_of(own_key, dims, cuts, least, largest):
    gain, own = 1.0, jax.random.fold_in(own_key, 6)
    for dim, blocks in cuts:
        heights = jnp.exp(jax.random.uniform(jax.random.fold_in(own, dim), (blocks,), jnp.float32, least / len(cuts), largest / len(cuts)))
        gain = gain * jnp.repeat(heights, dims[dim] // blocks).reshape([-1 if axis == dim else 1 for axis in range(len(dims))])
    return gain


def gaussian(rng, shape, deviation, reach, cuts=(), kind=jnp.bfloat16):
    values = deviation * jax.random.normal(rng, shape, jnp.float32)
    if cuts:
        values = values * level_of(rng, shape, cuts, -0.22, 0.18)
    return jnp.clip(values, -reach, reach).astype(kind)


def setup_inputs(seed: int = 0) -> dict:
    seeds = jax.random.split(jax.random.key(seed), 9)
    queries = draw_queries(jax.random.fold_in(seeds[8], 71), 0)
    keys = draw_keys(jax.random.fold_in(seeds[8], 71), 0)
    values = gaussian(seeds[2], (RESPONSES, LEN, KVH * HD), 1.0, 6.0, ((0, 32),))
    out_weight = gaussian(seeds[3], (HQ * HD, D), (HD // 8) ** -0.5, 1.5, ((1, 16),))
    order_bias = jnp.clip(jax.random.uniform(seeds[4], (2, HQ), jnp.float32, -2.0, 2.0), -2.0, 2.0)
    partners = draw_partners(jax.random.fold_in(seeds[8], 71), 0)
    count = draw_count(jax.random.fold_in(seeds[8], 71), 0)
    order = set_ends((jax.random.randint(seeds[7], (RESPONSES, SLOTS), 0, 2) < 1).astype(jnp.int32), jax.random.fold_in(seeds[7], 1), 0, 1)
    return {"queries": queries, "keys": keys, "values": values, "out_weight": out_weight, "order_bias": order_bias, "partners": partners, "count": count, "order": order}


def reference(queries, keys, values, out_weight, order_bias, partners, count, order):
    group_size = HQ // KVH
    score_scale = 1.0 / math.sqrt(HD)
    slot_ids = jnp.arange(SLOTS, dtype=jnp.int32)
    causal = jnp.arange(LEN)[:, None] >= jnp.arange(LEN)[None, :]

    def one_response(resp_id):
        query_rows = queries[resp_id].reshape(LEN, HQ, HD).astype(jnp.float32)
        picked = jnp.maximum(partners[resp_id], 0).astype(jnp.int32)
        in_use = slot_ids < count[resp_id]
        key_rows = jnp.concatenate([keys[resp_id][None], keys[picked]], 0).reshape(SLOTS + 1, LEN, KVH, HD)
        value_rows = jnp.concatenate([values[resp_id][None], values[picked]], 0).reshape(SLOTS + 1, LEN, KVH, HD)
        key_rows = jnp.repeat(key_rows, group_size, axis=2).astype(jnp.float32)
        value_rows = jnp.repeat(value_rows, group_size, axis=2).astype(jnp.float32)
        scores = jnp.einsum('ihd,sjhd->hisj', query_rows, key_rows) * score_scale
        slot_bias = order_bias[order[resp_id]]
        bias_all = jnp.concatenate([jnp.zeros((1, HQ), jnp.float32), slot_bias], 0).T
        scores = scores + bias_all[:, None, :, None]
        partner_seen = jnp.broadcast_to(in_use[None, :, None], (LEN, SLOTS, LEN))
        visible = jnp.concatenate([causal[:, None, :], partner_seen], 1)
        scores = jnp.where(visible[None], scores, -jnp.inf)
        highest = lax.optimization_barrier(jnp.max(scores, axis=(2, 3), keepdims=True))
        expo = jnp.exp(scores - highest)
        weights = (expo / lax.optimization_barrier(jnp.sum(expo, axis=(2, 3), keepdims=True))).astype(jnp.bfloat16)
        attended = jnp.einsum('hisj,sjhd->ihd', weights.astype(jnp.float32), value_rows).astype(jnp.bfloat16)
        attended = attended.reshape(LEN, HQ * HD)
        return jnp.dot(attended, out_weight, preferred_element_type=jnp.float32).astype(jnp.bfloat16)
    return lax.map(one_response, jnp.arange(RESPONSES, dtype=jnp.int32))
```

```python
import functools
import math

import jax
import jax.numpy as jnp
from jax import lax
from jax.experimental import pallas as pl
from jax.experimental.pallas import tpu as pltpu
from jax.sharding import PartitionSpec as P

HQ = 32
KVH = 4
HD = 128
REACH = 3
SLOTS = 6
LEN = 512
ROWS = 256
ONES = 16
MESH = pl.DeviceIdType.MESH
LOG2E = math.log2(math.e)
ABSENT = -1e30


def kernel(
    nr,
    nm,
    partners_ref,
    count_ref,
    order_ref,
    bias_ref,
    q_hbm,
    k_hbm,
    v_hbm,
    w_hbm,
    out_hbm,
    qs,
    kv,
    vraw,
    w,
    g,
    acc,
    o_acc,
    m_acc,
    outv,
    load_sem,
    kv_send,
    kv_recv,
    kvs_send,
    kvs_recv,
    g_send,
    g_recv,
    gs_send,
    gs_recv,
    out_sem,
):
    resp = lax.axis_index("resp")
    mp = lax.axis_index("mp")
    core = lax.rem(mp, 2)
    other = 1 - core
    kv_head = lax.div(mp * 2, HQ // KVH)
    r_next, r_prev = lax.rem(resp + 1, nr), lax.rem(resp + nr - 1, nr)
    z_next, z_prev = lax.rem(mp + 2, nm), lax.rem(mp + nm - 2, nm)
    sib = mp + 1 - 2 * core
    half_len = LEN // 2
    scale = LOG2E / math.sqrt(HD)

    columns = pl.ds(pl.multiple_of(kv_head * HD, HD), HD)
    load_k = pltpu.make_async_copy(k_hbm.at[0, :, columns], kv.at[0, 0], load_sem.at[0])
    load_v = pltpu.make_async_copy(v_hbm.at[0, :, columns], vraw, load_sem.at[1])
    load_v.start()
    load_k.start()
    load_q = []
    for chunk in range(4):
        head, part = chunk // 2, chunk % 2
        load_q.append(
            pltpu.make_async_copy(
                q_hbm.at[0, pl.ds(part * ROWS, ROWS), pl.ds(head * HD, HD)],
                qs.at[chunk],
                load_sem.at[2 + chunk],
            )
        )
        load_q[-1].start()
    load_w = pltpu.make_async_copy(w_hbm, w, load_sem.at[6])
    load_w.start()

    barrier = pltpu.get_barrier_semaphore()
    for device in ((r_next, mp), (r_prev, mp), (resp, z_next), (resp, z_prev), (resp, sib)):
        pl.semaphore_signal(barrier, inc=1, device_id=device, device_id_type=MESH)

    load_v.wait()
    for block in range(LEN // HD):
        rows = pl.ds(block * HD, HD)
        kv[0, 1, rows, :] = vraw[rows, :].T
    load_k.wait()
    pl.semaphore_wait(barrier, 5)

    def kv_copy(step, way, half):
        source = 0 if step == 1 else 1 + 2 * (step - 2) + way
        target = 1 + 2 * (step - 1) + way
        rows = pl.ds(half * half_len, half_len)
        index = (2 * (step - 1) + way) * 2 + half
        return pltpu.make_async_remote_copy(
            src_ref=kv.at[source, core, rows],
            dst_ref=kv.at[target, core, rows],
            send_sem=kv_send.at[index],
            recv_sem=kv_recv.at[index],
            device_id=((r_next, r_prev)[way], mp),
            device_id_type=MESH,
        )

    def kv_share(step, way, half, which):
        slot = 1 + 2 * (step - 1) + way
        rows = pl.ds(half * half_len, half_len)
        index = (2 * (step - 1) + way) * 2 + half
        return pltpu.make_async_remote_copy(
            src_ref=kv.at[slot, which, rows],
            dst_ref=kv.at[slot, which, rows],
            send_sem=kvs_send.at[index],
            recv_sem=kvs_recv.at[index],
            device_id=(resp, sib),
            device_id_type=MESH,
        )

    for half in range(2):
        for way in range(2):
            kv_copy(1, way, half).start()

    def pass_on(step, half):
        for way in range(2):
            kv_copy(step, way, half).wait_recv()
            if step < REACH:
                kv_copy(step + 1, way, half).start()
            kv_share(step, way, half, core).start()

    def from_sibling(step):
        for half in range(2):
            for way in range(2):
                kv_share(step, way, half, other).wait_recv()

    def offset_bias(step, way, head):
        name = lax.rem(resp + (nr - step if way == 0 else step), nr)
        low = bias_ref[0, 2 * mp + head] * LOG2E
        high = bias_ref[1, 2 * mp + head] * LOG2E
        result = jnp.float32(ABSENT)
        for slot in range(SLOTS):
            listed = (partners_ref[0, slot] == name) & (slot < count_ref[0])
            result = jnp.where(listed, jnp.where(order_ref[0, slot] == 1, high, low), result)
        return result

    def transposed_values(slot):
        blocks = [kv[slot, 1, pl.ds(b * HD, HD), :] for b in range(LEN // HD)]
        joined = jnp.concatenate(blocks, axis=1)
        return jnp.concatenate([joined, jnp.ones((ONES, LEN), jnp.bfloat16)], axis=0)

    def scores(keys, queries):
        return lax.dot_general(
            keys, queries, (((1,), (1,)), ((), ())), preferred_element_type=jnp.float32
        )

    for copy in load_q:
        copy.wait()

    def own_block(chunk, part):
        length = (part + 1) * ROWS
        s = scores(kv[0, 0, pl.ds(0, length), :], qs[chunk]) * scale
        key_pos = lax.broadcasted_iota(jnp.int32, (length, ROWS), 0)
        query_pos = lax.broadcasted_iota(jnp.int32, (length, ROWS), 1) + part * ROWS
        s = jnp.where(key_pos <= query_pos, s, ABSENT)
        top = jnp.max(s, axis=0, keepdims=True)
        p = jnp.exp2(s - top).astype(jnp.bfloat16)
        vt = transposed_values(0)[:, :length]
        m_acc[chunk] = jnp.broadcast_to(top, (8, ROWS))
        o_acc[chunk] = jnp.dot(vt, p, preferred_element_type=jnp.float32)

    def pair_block(step, chunk, bias0, bias1):
        first = 1 + 2 * (step - 1)
        queries = qs[chunk]
        s0 = scores(kv[first, 0], queries) * scale
        s1 = scores(kv[first + 1, 0], queries) * scale
        before = m_acc[chunk, 0:1, :]
        top = jnp.maximum(
            jnp.max(s0, axis=0, keepdims=True) + bias0, jnp.max(s1, axis=0, keepdims=True) + bias1
        )
        top = jnp.maximum(before, top)
        p0 = jnp.exp2(s0 - (top - bias0)).astype(jnp.bfloat16)
        p1 = jnp.exp2(s1 - (top - bias1)).astype(jnp.bfloat16)
        fresh = jnp.dot(transposed_values(first), p0, preferred_element_type=jnp.float32)
        fresh += jnp.dot(transposed_values(first + 1), p1, preferred_element_type=jnp.float32)
        m_acc[chunk] = jnp.broadcast_to(top, (8, ROWS))
        o_acc[chunk] = o_acc[chunk] * jnp.exp2(before - top) + fresh

    def finish(chunk):
        head, part = chunk // 2, chunk % 2
        total = o_acc[chunk]
        normal = total[:HD, :] * (1.0 / total[HD : HD + 1, :])
        g[2 * mp + head, pl.ds(part * ROWS, ROWS), :] = normal.T.astype(jnp.bfloat16)

    for chunk in range(4):
        own_block(chunk, chunk % 2)

    chips = nm // 2
    reach = (chips // 2, chips - 1 - chips // 2)

    def hops(way, head):
        return reach[0] if way == head else reach[1]

    def origin(way, hop):
        return lax.rem(mp + (nm - 2 * hop if way == 0 else 2 * hop), nm)

    def g_copy(hop, way, head):
        row = 2 * origin(way, hop - 1) + head
        index = ((hop - 1) * 2 + way) * 2 + head
        return pltpu.make_async_remote_copy(
            src_ref=g.at[row],
            dst_ref=g.at[row],
            send_sem=g_send.at[index],
            recv_sem=g_recv.at[index],
            device_id=(resp, (z_next, z_prev)[way]),
            device_id_type=MESH,
        )

    def g_arrival(hop, way, head):
        row = 2 * origin(way, hop) + head
        index = ((hop - 1) * 2 + way) * 2 + head
        return pltpu.make_async_remote_copy(
            src_ref=g.at[row],
            dst_ref=g.at[row],
            send_sem=g_send.at[index],
            recv_sem=g_recv.at[index],
            device_id=(resp, (z_next, z_prev)[way]),
            device_id_type=MESH,
        )

    def g_share(hop, way, head, sent):
        row = 2 * origin(way, hop) + head
        row = row if sent else row + 2 * (sib - mp)
        index = (hop * 2 + way) * 2 + head
        return pltpu.make_async_remote_copy(
            src_ref=g.at[row],
            dst_ref=g.at[row],
            send_sem=gs_send.at[index],
            recv_sem=gs_recv.at[index],
            device_id=(resp, sib),
            device_id_type=MESH,
        )

    for step in range(1, REACH + 1):
        pass_on(step, 0)
        pass_on(step, 1)
        from_sibling(step)
        for head in range(2):
            bias0, bias1 = offset_bias(step, 0, head), offset_bias(step, 1, head)
            for part in range(2):
                pair_block(step, head * 2 + part, bias0, bias1)
                if step == REACH:
                    finish(head * 2 + part)
            if step == REACH:
                g_copy(1, 0, head).start()
                g_copy(1, 1, head).start()
                g_share(0, 0, head, True).start()

    load_w.wait()

    def product(device, rows):
        left = jnp.concatenate([g[2 * device, rows, :], g[2 * device + 1, rows, :]], axis=1)
        right = w[pl.ds(pl.multiple_of(device * 2 * HD, 2 * HD), 2 * HD), :]
        return jnp.dot(left, right, preferred_element_type=jnp.float32)

    def add_product(device, first=False):
        for part in range(2):
            rows = pl.ds(part * ROWS, ROWS)
            if first:
                acc[rows, :] = product(device, rows)
            else:
                acc[rows, :] += product(device, rows)

    add_product(mp, True)
    pending = [(0, 0)]
    for hop in range(1, reach[0] + 1):
        later = []
        for head in range(2):
            for way in range(2):
                if hop > hops(way, head):
                    continue
                g_arrival(hop, way, head).wait_recv()
                if hop < hops(way, head):
                    g_copy(hop + 1, way, head).start()
                g_share(hop, way, head, True).start()
        if hop < reach[0]:
            for way, back in pending:
                for head in range(2):
                    g_share(back, way, head, False).wait_recv()
                add_product(origin(way, back) + sib - mp)
            for way in range(2):
                add_product(origin(way, hop))
            pending = [(0, hop), (1, hop)]
    for way, back in pending:
        for head in range(2):
            g_share(back, way, head, False).wait_recv()
        add_product(origin(way, back) + sib - mp)
    add_product(origin(0, reach[0]))
    for way in range(2):
        g_share(reach[0], way, way, False).wait_recv()
    last = origin(0, reach[0]) + sib - mp
    stores = []
    for part in range(2):
        rows = pl.ds(part * ROWS, ROWS)
        outv[rows, :] = (acc[rows, :] + product(last, rows)).astype(jnp.bfloat16)
        stores.append(pltpu.make_async_copy(outv.at[rows], out_hbm.at[0, rows], out_sem.at[part]))
        stores[-1].start()

    for step in range(1, REACH + 1):
        for half in range(2):
            for way in range(2):
                kv_copy(step, way, half).wait_send()
                kv_share(step, way, half, core).wait_send()
    for head in range(2):
        g_share(0, 0, head, True).wait_send()
        for way in range(2):
            for hop in range(1, hops(way, head) + 1):
                g_copy(hop, way, head).wait_send()
                g_share(hop, way, head, True).wait_send()
    for copy in stores:
        copy.wait()


def on_device(queries, keys, values, out_weight, order_bias, partners, count, order):
    nr, nm = lax.axis_size("resp"), lax.axis_size("mp")
    smem = pl.BlockSpec(memory_space=pltpu.SMEM)
    anywhere = pl.BlockSpec(memory_space=pl.ANY)
    seq_len = queries.shape[1]
    width = out_weight.shape[1]
    kv_copies = 4 * REACH
    hop_copies = 4 * (nm // 4)
    return pl.pallas_call(
        functools.partial(kernel, nr, nm),
        out_shape=jax.ShapeDtypeStruct((1, seq_len, width), jnp.bfloat16),
        in_specs=[smem] * 4 + [anywhere] * 4,
        out_specs=anywhere,
        scratch_shapes=[
            pltpu.VMEM((4, ROWS, HD), jnp.bfloat16),
            pltpu.VMEM((1 + 2 * REACH, 2, LEN, HD), jnp.bfloat16),
            pltpu.VMEM((LEN, HD), jnp.bfloat16),
            pltpu.VMEM(out_weight.shape, jnp.bfloat16),
            pltpu.VMEM((HQ, LEN, HD), jnp.bfloat16),
            pltpu.VMEM((seq_len, width), jnp.float32),
            pltpu.VMEM((4, HD + ONES, ROWS), jnp.float32),
            pltpu.VMEM((4, 8, ROWS), jnp.float32),
            pltpu.VMEM((seq_len, width), jnp.bfloat16),
            pltpu.SemaphoreType.DMA((7,)),
            pltpu.SemaphoreType.DMA((kv_copies,)),
            pltpu.SemaphoreType.DMA((kv_copies,)),
            pltpu.SemaphoreType.DMA((kv_copies,)),
            pltpu.SemaphoreType.DMA((kv_copies,)),
            pltpu.SemaphoreType.DMA((hop_copies,)),
            pltpu.SemaphoreType.DMA((hop_copies,)),
            pltpu.SemaphoreType.DMA((hop_copies + 4,)),
            pltpu.SemaphoreType.DMA((hop_copies + 4,)),
            pltpu.SemaphoreType.DMA((2,)),
        ],
        compiler_params=pltpu.CompilerParams(
            collective_id=0, has_side_effects=True, vmem_limit_bytes=56 * 1024 * 1024
        ),
    )(partners, count, order, order_bias, queries, keys, values, out_weight)


def solution(mesh):
    in_specs = (
        P("resp", None, "mp"),
        P("resp", None, None),
        P("resp", None, None),
        P(None, "mp"),
        P(),
        P("resp", None),
        P("resp"),
        P("resp", None),
    )
    out_specs = P("resp", None, "mp")
    return jax.shard_map(
        on_device, mesh=mesh, in_specs=in_specs, out_specs=out_specs, check_vma=False
    )
```
